32 devices in a mesh: layer: 4 (over y, core), latent: 8 (over z, x).
Axes of the slice: x: 2, y: 2, z: 4, core: 2. Of those that a mesh axis runs over, the one named last changes fastest.
Arguments:
- inputs: bfloat16 [4, 128, 4096], P('layer', 'latent'), may hold values from -6 to 6
- targets: bfloat16 [4, 128, 4096], P('layer', 'latent'), may hold values from -6 to 6
- w_enc: bfloat16 [4, 4096, 8192], P('layer', None, 'latent'), may hold values from -0.09375 to 0.09375
- b_enc: float32 [4, 8192], P('layer', 'latent'), may hold values from -3 to 3
- w_dec: bfloat16 [4, 4, 8192, 4096], P('layer', None, 'latent'), may hold values from -0.03125 to 0.03125
- b_dec: float32 [4, 4096], P('layer'), may hold values from -3 to 3
Outputs:
- grad_enc: bfloat16 [4, 4096, 8192], P('layer', None, 'latent')
- grad_benc: float32 [4, 8192], P('layer', 'latent')
- grad_dec: bfloat16 [4, 4, 8192, 4096], P('layer', None, 'latent')
- grad_bdec: float32 [4, 4096], P('layer')
The draws below stay inside these ranges and needn't reach their ends.
All inputs are finite; a program needn't handle non-finite values.
Results may differ from the reference program's by a relative error of at most 0.0057.
Values may be sent and summed in bfloat16 or wider, within the bound.
A program may use at most 192 MiB of HBM per device.

```python
import jax
import jax.numpy as jnp
from jax import lax

D = 4096
LATENTS = 8192
TOKENS = 128
LAYERS = 4


def levels(rng, dims, cuts, least, high):
    factor_of = 1.0
    for axis_at, blocks in cuts:
        draws = jax.random.uniform(jax.random.fold_in(jax.random.fold_in(rng, 6), axis_at), (blocks,), jnp.float32, least / len(cuts), high / len(cuts))
        factor_of = factor_of * jnp.repeat(jnp.exp(draws), dims[axis_at] // blocks).reshape((-1,) + (1,) * (len(dims) - 1 - axis_at))
    return factor_of


def scatter_about(own_key, shape, width, most, cuts=(), dtype=jnp.bfloat16):
    result = width * jax.random.normal(own_key, shape, jnp.float32)
    if cuts:
        result = result * levels(own_key, shape, cuts, -0.22, 0.18)
    return jnp.clip(result, -most, most).astype(dtype)


def setup_inputs(seed: int = 0) -> dict:
    seeds = jax.random.split(jax.random.key(seed), 7)
    inputs = scatter_about(seeds[0], (LAYERS, TOKENS, D), 1.0, 6.0, ((0, 4), (1, 8)))
    targets = scatter_about(seeds[1], (LAYERS, TOKENS, D), 1.0, 6.0, ((0, 4), (1, 8)))
    w_enc = scatter_about(seeds[2], (LAYERS, D, LATENTS), D ** -0.5, 0.09375, ((0, 4), (2, 8)))
    b_enc = scatter_about(seeds[3], (LAYERS, LATENTS), 0.5, 3.0, ((0, 4), (1, 8)), jnp.float32)
    w_dec = scatter_about(seeds[4], (LAYERS, LAYERS, LATENTS, D), (LAYERS * LATENTS) ** -0.5, 0.03125, ((0, 4), (2, 8)))
    b_dec = scatter_about(seeds[5], (LAYERS, D), 0.5, 3.0, ((0, 4),), jnp.float32)
    return {"inputs": inputs, "targets": targets, "w_enc": w_enc, "b_enc": b_enc, "w_dec": w_dec, "b_dec": b_dec}


penalty = 0.5
eps = 1e-06

def reference(inputs, targets, w_enc, b_enc, w_dec, b_dec):
    pres = []
    acts = []
    for s in range(LAYERS):
        pre = jnp.dot(inputs[s], w_enc[s], preferred_element_type=jnp.float32) + b_enc[s]
        pres.append(pre)
        positive = jnp.maximum(pre, 0.0)
        acts.append((positive * positive).astype(jnp.bfloat16))
    err_low = []
    bias_rows = []
    for t in range(LAYERS):
        recon = jnp.zeros((TOKENS, D), jnp.float32)
        for s in range(t + 1):
            recon = recon + jnp.dot(acts[s], w_dec[s, t], preferred_element_type=jnp.float32)
        error = recon + b_dec[t] - targets[t].astype(jnp.float32)
        bias_rows.append(lax.optimization_barrier(jnp.sum(error, axis=0)))
        err_low.append(error.astype(jnp.bfloat16))
    grad_enc = []
    grad_benc = []
    grad_dec = []
    for s in range(LAYERS):
        total_sq = jnp.zeros((LATENTS,), jnp.float32)
        back = jnp.zeros((TOKENS, LATENTS), jnp.float32)
        for t in range(s, LAYERS):
            wide = w_dec[s, t].astype(jnp.float32)
            total_sq = total_sq + lax.optimization_barrier(jnp.sum(wide * wide, axis=1))
            back = back + lax.dot_general(err_low[t], w_dec[s, t], (((1,), (1,)), ((), ())), preferred_element_type=jnp.float32)
        norms = jnp.sqrt(total_sq + eps)
        d_act = back + penalty * norms[None, :]
        d_pre = d_act * 2.0 * jnp.maximum(pres[s], 0.0)
        grad_benc.append(lax.optimization_barrier(jnp.sum(d_pre, axis=0)))
        d_low = d_pre.astype(jnp.bfloat16)
        grad_enc.append(lax.dot_general(inputs[s], d_low, (((0,), (0,)), ((), ())), preferred_element_type=jnp.float32).astype(jnp.bfloat16))
        act_total = lax.optimization_barrier(jnp.sum(acts[s].astype(jnp.float32), axis=0))
        scale = penalty * act_total / norms
        rows = []
        for t in range(LAYERS):
            if t < s:
                rows.append(jnp.zeros((LATENTS, D), jnp.bfloat16))
            else:
                mse = lax.dot_general(acts[s], err_low[t], (((0,), (0,)), ((), ())), preferred_element_type=jnp.float32)
                rows.append((mse + scale[:, None] * w_dec[s, t].astype(jnp.float32)).astype(jnp.bfloat16))
        grad_dec.append(jnp.stack(rows))
    return (jnp.stack(grad_enc), jnp.stack(grad_benc), jnp.stack(grad_dec), jnp.stack(bias_rows))
```

```python
import functools

import jax
import jax.numpy as jnp
from jax import lax
from jax.experimental import pallas as pl
from jax.experimental.pallas import tpu as pltpu
from jax.sharding import PartitionSpec as P

penalty = 0.5
eps = 1e-06
f32 = jnp.float32
bf16 = jnp.bfloat16
VMEM_LIMIT = 60 * 1024 * 1024


def forward_kernel(src, whole, w_enc, b_enc, w_dec, positive, act, partial, total):
    step = pl.program_id(0)
    depth = w_dec.shape[0]
    features = w_dec.shape[2]
    cols = min(features, 1024)

    @pl.when(step == 0)
    def _():
        total[...] = jnp.zeros_like(total)

    pre = jnp.dot(whole[...], w_enc[...], preferred_element_type=f32) + b_enc[...]
    pos = jnp.maximum(pre, 0.0)
    positive[...] = pos
    act[...] = (pos * pos).astype(bf16)
    for t in range(depth):

        @pl.when(t >= src[0])
        def _():
            for c in range(0, features, cols):
                total[t, :, c : c + cols] += jnp.dot(
                    act[...], w_dec[t, :, c : c + cols], preferred_element_type=f32
                )

    @pl.when(step == pl.num_programs(0) - 1)
    def _():
        for t in range(depth):
            partial[t] = total[t].astype(partial.dtype)


def forward(src, whole, w_enc, b_enc, w_dec, out_dtype):
    tokens, features = whole.shape
    depth, latents, _ = w_dec.shape
    block = min(latents, 256)
    return pl.pallas_call(
        forward_kernel,
        grid_spec=pltpu.PrefetchScalarGridSpec(
            num_scalar_prefetch=1,
            grid=(latents // block,),
            in_specs=[
                pl.BlockSpec((tokens, features), lambda i, s: (0, 0), pipeline_mode=pl.Buffered(1)),
                pl.BlockSpec((features, block), lambda i, s: (0, i)),
                pl.BlockSpec((1, block), lambda i, s: (0, i)),
                pl.BlockSpec((depth, block, features), lambda i, s: (0, i, 0)),
            ],
            out_specs=[
                pl.BlockSpec((tokens, block), lambda i, s: (0, i)),
                pl.BlockSpec((tokens, block), lambda i, s: (0, i)),
                pl.BlockSpec((depth, tokens, features), lambda i, s: (0, 0, 0), pipeline_mode=pl.Buffered(1)),
            ],
            scratch_shapes=[pltpu.VMEM((depth, tokens, features), f32)],
        ),
        out_shape=[
            jax.ShapeDtypeStruct((tokens, latents), f32),
            jax.ShapeDtypeStruct((tokens, latents), bf16),
            jax.ShapeDtypeStruct((depth, tokens, features), out_dtype),
        ],
        compiler_params=pltpu.CompilerParams(
            dimension_semantics=("arbitrary",), vmem_limit_bytes=VMEM_LIMIT
        ),
    )(src, whole, w_enc, b_enc, w_dec)


def backward_kernel(
    src, whole, positive, act, errors, w_dec, grad_enc, grad_benc, grad_dec, flipped, back, squares
):
    depth, block, features = w_dec.shape
    cols = min(features, 512)
    lanes = 128

    @pl.when(pl.program_id(0) == 0)
    def _():
        flipped[...] = whole[...].T

    back[...] = jnp.zeros_like(back)
    squares[...] = jnp.zeros_like(squares)
    for t in range(depth):

        @pl.when(t >= src[0])
        def _():
            back[...] += lax.dot_general(
                errors[t], w_dec[t], (((1,), (1,)), ((), ())), preferred_element_type=f32
            )
            partial = squares[...]
            for c in range(0, features, lanes):
                wide = w_dec[t, :, c : c + lanes].astype(f32)
                partial = partial + wide * wide
            squares[...] = partial

    sums = squares[...]
    norm_row = jnp.sqrt(jnp.sum(sums.T, axis=0, keepdims=True) + eps)
    norm_col = jnp.sqrt(jnp.sum(sums, axis=1, keepdims=True) + eps)
    d_pre = (back[...] + penalty * norm_row) * 2.0 * positive[...]
    grad_benc[...] = jnp.sum(d_pre, axis=0, keepdims=True)
    grad_enc[...] = jnp.dot(
        flipped[...], d_pre.astype(bf16), preferred_element_type=f32
    ).astype(bf16)
    turned = act[...].astype(f32).T
    scale = penalty * jnp.sum(turned, axis=1, keepdims=True) / norm_col
    turned = turned.astype(bf16)
    for t in range(depth):

        @pl.when(t >= src[0])
        def _():
            for c in range(0, features, cols):
                mse = jnp.dot(turned, errors[t, :, c : c + cols], preferred_element_type=f32)
                grad_dec[t, :, c : c + cols] = (
                    mse + scale * w_dec[t, :, c : c + cols].astype(f32)
                ).astype(bf16)

        @pl.when(t < src[0])
        def _():
            grad_dec[t] = jnp.zeros_like(grad_dec[t])


def backward(src, whole, positive, act, errors, w_dec):
    tokens, features = whole.shape
    depth, latents, _ = w_dec.shape
    block = min(latents, 128)
    return pl.pallas_call(
        backward_kernel,
        grid_spec=pltpu.PrefetchScalarGridSpec(
            num_scalar_prefetch=1,
            grid=(latents // block,),
            in_specs=[
                pl.BlockSpec((tokens, features), lambda i, s: (0, 0), pipeline_mode=pl.Buffered(1)),
                pl.BlockSpec((tokens, block), lambda i, s: (0, i)),
                pl.BlockSpec((tokens, block), lambda i, s: (0, i)),
                pl.BlockSpec((depth, tokens, features), lambda i, s: (0, 0, 0), pipeline_mode=pl.Buffered(1)),
                pl.BlockSpec((depth, block, features), lambda i, s: (0, i, 0)),
            ],
            out_specs=[
                pl.BlockSpec((features, block), lambda i, s: (0, i)),
                pl.BlockSpec((1, block), lambda i, s: (0, i)),
                pl.BlockSpec((depth, block, features), lambda i, s: (0, i, 0)),
            ],
            scratch_shapes=[
                pltpu.VMEM((features, tokens), bf16),
                pltpu.VMEM((tokens, block), f32),
                pltpu.VMEM((block, 128), f32),
            ],
        ),
        out_shape=[
            jax.ShapeDtypeStruct((features, latents), bf16),
            jax.ShapeDtypeStruct((1, latents), f32),
            jax.ShapeDtypeStruct((depth, latents, features), bf16),
        ],
        compiler_params=pltpu.CompilerParams(
            dimension_semantics=("arbitrary",), vmem_limit_bytes=VMEM_LIMIT
        ),
    )(src, whole, positive, act, errors, w_dec)


def local(inputs, targets, w_enc, b_enc, w_dec, b_dec):
    src = lax.axis_index("layer").astype(jnp.int32)[None]
    whole = lax.all_gather(inputs[0], "latent", axis=0, tiled=True)
    positive, act, partial = forward(src, whole, w_enc[0], b_enc, w_dec[0], f32)
    spread = lax.psum_scatter(partial, "layer", scatter_dimension=0, tiled=True)
    recon = lax.psum_scatter(spread, "latent", scatter_dimension=1, tiled=True)
    error = recon[0] + b_dec[0] - targets[0].astype(f32)
    err_low = error.astype(bf16)[None]
    stacked = lax.all_gather(err_low, "latent", axis=1, tiled=True)
    errors = lax.all_gather(stacked, "layer", axis=0, tiled=True)
    grad_bdec = lax.psum(jnp.sum(error, axis=0), "latent")[None, :]
    grad_enc, grad_benc, grad_dec = backward(src, whole, positive, act, errors, w_dec[0])
    return (grad_enc[None], grad_benc, grad_dec[None], grad_bdec)


def solution(mesh):
    placed = (
        P("layer", "latent", None),
        P("layer", "latent", None),
        P("layer", None, "latent"),
        P("layer", "latent"),
        P("layer", None, "latent", None),
        P("layer", None),
    )
    return jax.shard_map(
        local,
        mesh=mesh,
        in_specs=placed,
        out_specs=(
            P("layer", None, "latent"),
            P("layer", "latent"),
            P("layer", None, "latent", None),
            P("layer", None),
        ),
        check_vma=False,
    )
```

```python
import functools

import jax
import jax.numpy as jnp
from jax import lax
from jax.experimental import pallas as pl
from jax.experimental.pallas import tpu as pltpu
from jax.sharding import PartitionSpec as P

penalty = 0.5
eps = 1e-06
f32 = jnp.float32
bf16 = jnp.bfloat16
VMEM_LIMIT = 60 * 1024 * 1024


def forward_kernel(src, whole, w_enc, b_enc, w_dec, positive, act, partial, total):
    step = pl.program_id(0)
    depth = w_dec.shape[0]
    features = w_dec.shape[2]
    cols = min(features, 1024)

    @pl.when(step == 0)
    def _():
        total[...] = jnp.zeros_like(total)

    pre = jnp.dot(whole[...], w_enc[...], preferred_element_type=f32) + b_enc[...]
    pos = jnp.maximum(pre, 0.0)
    positive[...] = pos
    act[...] = (pos * pos).astype(bf16)
    for t in range(depth):

        @pl.when(t >= src[0])
        def _():
            for c in range(0, features, cols):
                total[t, :, c : c + cols] += jnp.dot(
                    act[...], w_dec[t, :, c : c + cols], preferred_element_type=f32
                )

    @pl.when(step == pl.num_programs(0) - 1)
    def _():
        for t in range(depth):
            partial[t] = total[t].astype(partial.dtype)


def forward(src, whole, w_enc, b_enc, w_dec, out_dtype):
    tokens, features = whole.shape
    depth, latents, _ = w_dec.shape
    block = min(latents, 256)
    return pl.pallas_call(
        forward_kernel,
        grid_spec=pltpu.PrefetchScalarGridSpec(
            num_scalar_prefetch=1,
            grid=(latents // block,),
            in_specs=[
                pl.BlockSpec((tokens, features), lambda i, s: (0, 0), pipeline_mode=pl.Buffered(1)),
                pl.BlockSpec((features, block), lambda i, s: (0, i)),
                pl.BlockSpec((1, block), lambda i, s: (0, i)),
                pl.BlockSpec((depth, block, features), lambda i, s: (0, i, 0)),
            ],
            out_specs=[
                pl.BlockSpec((tokens, block), lambda i, s: (0, i)),
                pl.BlockSpec((tokens, block), lambda i, s: (0, i)),
                pl.BlockSpec((depth, tokens, features), lambda i, s: (0, 0, 0), pipeline_mode=pl.Buffered(1)),
            ],
            scratch_shapes=[pltpu.VMEM((depth, tokens, features), f32)],
        ),
        out_shape=[
            jax.ShapeDtypeStruct((tokens, latents), f32),
            jax.ShapeDtypeStruct((tokens, latents), bf16),
            jax.ShapeDtypeStruct((depth, tokens, features), out_dtype),
        ],
        compiler_params=pltpu.CompilerParams(
            dimension_semantics=("arbitrary",), vmem_limit_bytes=VMEM_LIMIT
        ),
    )(src, whole, w_enc, b_enc, w_dec)


def backward_kernel(
    src, whole, positive, act, errors, w_dec, grad_enc, grad_benc, grad_dec, flipped, back, squares
):
    depth, block, features = w_dec.shape
    cols = min(features, 512)
    lanes = 128

    @pl.when(pl.program_id(0) == 0)
    def _():
        flipped[...] = whole[...].T

    back[...] = jnp.zeros_like(back)
    squares[...] = jnp.zeros_like(squares)
    for t in range(depth):

        @pl.when(t >= src[0])
        def _():
            back[...] += lax.dot_general(
                errors[t], w_dec[t], (((1,), (1,)), ((), ())), preferred_element_type=f32
            )
            partial = squares[...]
            for c in range(0, features, lanes):
                wide = w_dec[t, :, c : c + lanes].astype(f32)
                partial = partial + wide * wide
            squares[...] = partial

    sums = squares[...]
    norm_row = jnp.sqrt(jnp.sum(sums.T, axis=0, keepdims=True) + eps)
    norm_col = jnp.sqrt(jnp.sum(sums, axis=1, keepdims=True) + eps)
    d_pre = (back[...] + penalty * norm_row) * 2.0 * positive[...]
    grad_benc[...] = jnp.sum(d_pre, axis=0, keepdims=True)
    grad_enc[...] = jnp.dot(
        flipped[...], d_pre.astype(bf16), preferred_element_type=f32
    ).astype(bf16)
    turned = act[...].astype(f32).T
    scale = penalty * jnp.sum(turned, axis=1, keepdims=True) / norm_col
    turned = turned.astype(bf16)
    for t in range(depth):

        @pl.when(t >= src[0])
        def _():
            for c in range(0, features, cols):
                mse = jnp.dot(turned, errors[t, :, c : c + cols], preferred_element_type=f32)
                grad_dec[t, :, c : c + cols] = (
                    mse + scale * w_dec[t, :, c : c + cols].astype(f32)
                ).astype(bf16)

        @pl.when(t < src[0])
        def _():
            grad_dec[t] = jnp.zeros_like(grad_dec[t])


def backward(src, whole, positive, act, errors, w_dec):
    tokens, features = whole.shape
    depth, latents, _ = w_dec.shape
    block = min(latents, 128)
    return pl.pallas_call(
        backward_kernel,
        grid_spec=pltpu.PrefetchScalarGridSpec(
            num_scalar_prefetch=1,
            grid=(latents // block,),
            in_specs=[
                pl.BlockSpec((tokens, features), lambda i, s: (0, 0), pipeline_mode=pl.Buffered(1)),
                pl.BlockSpec((tokens, block), lambda i, s: (0, i)),
                pl.BlockSpec((tokens, block), lambda i, s: (0, i)),
                pl.BlockSpec((depth, tokens, features), lambda i, s: (0, 0, 0), pipeline_mode=pl.Buffered(1)),
                pl.BlockSpec((depth, block, features), lambda i, s: (0, i, 0)),
            ],
            out_specs=[
                pl.BlockSpec((features, block), lambda i, s: (0, i)),
                pl.BlockSpec((1, block), lambda i, s: (0, i)),
                pl.BlockSpec((depth, block, features), lambda i, s: (0, i, 0)),
            ],
            scratch_shapes=[
                pltpu.VMEM((features, tokens), bf16),
                pltpu.VMEM((tokens, block), f32),
                pltpu.VMEM((block, 128), f32),
            ],
        ),
        out_shape=[
            jax.ShapeDtypeStruct((features, latents), bf16),
            jax.ShapeDtypeStruct((1, latents), f32),
            jax.ShapeDtypeStruct((depth, latents, features), bf16),
        ],
        compiler_params=pltpu.CompilerParams(
            dimension_semantics=("arbitrary",), vmem_limit_bytes=VMEM_LIMIT
        ),
    )(src, whole, positive, act, errors, w_dec)


MESH = pl.DeviceIdType.MESH


def place():
    layer, latent = lax.axis_index("layer"), lax.axis_index("latent")
    return layer // 2, lax.rem(layer, 2), latent // 2, lax.rem(latent, 2)


def remote(src, dst, send, recv, target):
    return pltpu.make_async_remote_copy(
        src_ref=src, dst_ref=dst, send_sem=send, recv_sem=recv, device_id=target, device_id_type=MESH
    )


def greet(partners):
    barrier = pltpu.get_barrier_semaphore()
    for partner in partners:
        pl.semaphore_signal(barrier, inc=1, device_id=partner, device_id_type=MESH)
    pl.semaphore_wait(barrier, len(partners))


def gather_kernel(rows, own, whole, send_z, recv_z, send_x, recv_x):
    y, c, z, x = place()
    layer = 2 * y + c
    mine = 2 * z + x
    beside = (layer, 2 * z + 1 - x)
    along = [(layer, 2 * lax.rem(z + d, rows) + x) for d in range(rows)]
    greet([beside] + along[1:])
    sent = []
    order = sorted(range(1, rows), key=lambda d: abs(2 * d - rows))
    for d in order:
        copy = remote(own, whole.at[mine], send_z.at[d], recv_z.at[d], along[d])
        copy.start()
        sent.append(copy)
    first = remote(own, whole.at[mine], send_x.at[0], recv_x.at[0], beside)
    first.start()
    whole[mine] = own[...]
    across = [first]
    for d in range(1, rows):
        start = 2 * lax.rem(z + rows - d, rows) + x
        remote(own, whole.at[start], send_z.at[d], recv_z.at[d], along[d]).wait_recv()
        copy = remote(whole.at[start], whole.at[start], send_x.at[d], recv_x.at[d], beside)
        copy.start()
        across.append(copy)
    for copy in sent:
        copy.wait_send()
    for copy in across:
        copy.wait()


def gather(block, peers):
    tokens, features = block.shape
    rows = peers // 2
    dma = pltpu.SemaphoreType.DMA((rows,))
    return pl.pallas_call(
        functools.partial(gather_kernel, rows),
        out_shape=jax.ShapeDtypeStruct((peers, tokens, features), bf16),
        in_specs=[pl.BlockSpec(memory_space=pltpu.VMEM)],
        out_specs=pl.BlockSpec(memory_space=pltpu.VMEM),
        scratch_shapes=[dma] * 4,
        compiler_params=pltpu.CompilerParams(collective_id=0, has_side_effects=True),
    )(block).reshape(peers * tokens, features)


def exchange_kernel(
    rows, part, targets, b_dec, errors, grad_bdec,
    core_in, out_x, in_x, out_z, in_z, own, out_y, in_y, biases,
    send_c, recv_c, send_x, recv_x, send_z, recv_z, send_y, recv_y,
    send_ez, recv_ez, send_ex, recv_ex, send_ec, recv_ec, send_b, recv_b,
):
    y, c, z, x = place()
    layer = 2 * y + c
    mine = 2 * z + x
    peers = 2 * rows
    core = (2 * y + 1 - c, mine)
    beside = (layer, 2 * z + 1 - x)
    across = (2 * (1 - y) + c, mine)
    along = [(layer, 2 * lax.rem(z + d, rows) + x) for d in range(rows)]
    everyone = [(layer, lax.rem(mine + o, peers)) for o in range(peers)]
    greet([core, across] + everyone[1:])
    bottom, top = y == 0, y == 1

    def only(k, body):
        if k == 1:
            body()
        else:
            pl.when(bottom)(body)

    def pair(d):
        return pl.ds(2 * lax.rem(z + d, rows), 2)

    def core_copy(k, d):
        return remote(
            part.at[1 - c + 2 * k, pair(d)], core_in.at[k, pair(d)], send_c.at[k, d], recv_c.at[k, d], core
        )

    def x_copy(k, d):
        return remote(out_x.at[k, d], in_x.at[k, d], send_x.at[k, d], recv_x.at[k, d], beside)

    def z_copy(k, d):
        return remote(out_z.at[k, d], in_z.at[k, d], send_z.at[k, d], recv_z.at[k, d], along[d])

    def both(k, at):
        return part[c + 2 * k, at].astype(f32) + core_in[k, at].astype(f32)

    def first(k, d):
        def body():
            core_copy(k, d).wait_recv()
            at = 2 * lax.rem(z + d, rows) + 1 - x
            out_x[k, d] = both(k, at).astype(bf16)
            x_copy(k, d).start()

        only(k, body)

    def second(k, d):
        def body():
            x_copy(k, d).wait_recv()
            at = 2 * lax.rem(z + d, rows) + x
            value = both(k, at) + in_x[k, d].astype(f32)
            if d == 0:
                own[k] = value
            else:
                out_z[k, d] = value.astype(bf16)
                z_copy(k, d).start()

        only(k, body)

    def collect(k):
        value = own[k]
        for d in range(1, rows):
            z_copy(k, d).wait_recv()
            value = value + in_z[k, d].astype(f32)
        return value

    def bias_copy(o):
        return remote(biases.at[mine], biases.at[mine], send_b.at[o], recv_b.at[o], everyone[o])

    def settle(value, k):
        error = value + b_dec[...] - targets[...].astype(f32)
        errors[c + 2 * k, mine] = error.astype(bf16)
        total = jnp.sum(error, axis=0, keepdims=True)
        width = total.shape[1] // 8
        for i in range(8):
            biases[mine, i : i + 1, :] = total[:, i * width : (i + 1) * width]

    up = remote(out_y, in_y, send_y.at[0], recv_y.at[0], across)
    high = errors.at[c + 2, mine]
    down = remote(high, high, send_y.at[1], recv_y.at[1], across)

    def spread_z(k, d):
        ref = errors.at[c + 2 * k, mine]
        return remote(ref, ref, send_ez.at[k, d], recv_ez.at[k, d], along[d])

    def spread_x(k, d):
        ref = errors.at[c + 2 * k, 2 * lax.rem(z + rows - d, rows) + x]
        return remote(ref, ref, send_ex.at[k, d], recv_ex.at[k, d], beside)

    def spread_c(k, d, side):
        ref = errors.at[side + 2 * k, pl.ds(2 * lax.rem(z + rows - d, rows), 2)]
        return remote(ref, ref, send_ec.at[k, d], recv_ec.at[k, d], core)

    def launch(k):
        for d in list(range(rows // 2, 0, -1)) + list(range(rows // 2 + 1, rows)):
            spread_z(k, d).start()
        spread_x(k, 0).start()

    units = [(k, d) for k in (1, 0) for d in list(range(1, rows)) + [0]]
    for k, d in units:
        only(k, core_copy(k, d).start)
    lag = 2
    for i in range(len(units) + lag):
        if i < len(units):
            first(*units[i])
        if i >= lag:
            second(*units[i - lag])
        if i == len(units) - 1:

            @pl.when(bottom)
            def _():
                out_y[...] = collect(1).astype(bf16)
                up.start()

            @pl.when(top)
            def _():
                value = collect(1)
                up.wait_recv()
                settle(value + in_y[...].astype(f32), 1)
                down.start()
                launch(1)

    @pl.when(bottom)
    def _():
        settle(collect(0), 0)
        launch(0)
        down.wait_recv()
        launch(1)

    for o in range(1, peers):
        bias_copy(o).start()

    for k in (0, 1):

        def relay(k=k):
            for d in range(1, rows):
                spread_z(k, d).wait_recv()
                spread_x(k, d).start()

        only(k, relay)

    forwards = {1: jnp.logical_or(bottom, c == 1), 0: jnp.logical_and(bottom, c == 1)}
    receives = {1: jnp.logical_or(bottom, c == 0), 0: jnp.logical_and(bottom, c == 0)}
    for k in (0, 1):

        def finish(k=k):
            for d in range(rows):
                spread_x(k, d).wait_recv()

                @pl.when(forwards[k])
                def _():
                    spread_c(k, d, c).start()

        only(k, finish)

    for o in range(1, peers):
        bias_copy(o).wait()
    total = biases[0]
    for i in range(1, peers):
        total = total + biases[i]
    grad_bdec[...] = total

    for k in (0, 1):

        @pl.when(receives[k])
        def _():
            for d in range(rows):
                spread_c(k, d, 1 - c).wait_recv()

        @pl.when(forwards[k])
        def _():
            for d in range(rows):
                spread_c(k, d, c).wait_send()

        def drain(k=k):
            for d in range(rows):
                core_copy(k, d).wait_send()
                x_copy(k, d).wait_send()
                spread_x(k, d).wait_send()
                if d:
                    z_copy(k, d).wait_send()
                    spread_z(k, d).wait_send()

        only(k, drain)

    pl.when(bottom)(up.wait_send)
    pl.when(top)(down.wait_send)


def exchange(partial, targets, b_dec, peers):
    depth, tokens, features = partial.shape
    rows = peers // 2
    chunk = tokens // peers
    slots = pltpu.VMEM((2, rows, chunk, features), bf16)
    dma = pltpu.SemaphoreType.DMA((2, rows))
    flat = pltpu.SemaphoreType.DMA((peers,))
    errors, grad_bdec = pl.pallas_call(
        functools.partial(exchange_kernel, rows),
        out_shape=[
            jax.ShapeDtypeStruct((depth, peers, chunk, features), bf16),
            jax.ShapeDtypeStruct((8, features // 8), f32),
        ],
        in_specs=[pl.BlockSpec(memory_space=pltpu.VMEM)] * 3,
        out_specs=[pl.BlockSpec(memory_space=pltpu.VMEM)] * 2,
        scratch_shapes=[
            pltpu.VMEM((2, peers, chunk, features), bf16),
            slots, slots, slots, slots,
            pltpu.VMEM((2, chunk, features), f32),
            pltpu.VMEM((chunk, features), bf16),
            pltpu.VMEM((chunk, features), bf16),
            pltpu.VMEM((peers, 8, features // 8), f32),
        ] + [dma] * 6 + [pltpu.SemaphoreType.DMA((2,))] * 2 + [dma] * 6 + [flat] * 2,
        compiler_params=pltpu.CompilerParams(
            collective_id=1, has_side_effects=True, vmem_limit_bytes=VMEM_LIMIT
        ),
    )(partial.reshape(depth, peers, chunk, features), targets, b_dec)
    return errors.reshape(depth, tokens, features), grad_bdec.reshape(1, features)


def paired(depth, peers, chunk, features):
    layers = lax.axis_size("layer")
    return layers == depth == 4 and peers % 2 == 0 and chunk % 16 == 0 and features % 1024 == 0


def local(inputs, targets, w_enc, b_enc, w_dec, b_dec):
    src = lax.axis_index("layer").astype(jnp.int32)[None]
    peers = lax.axis_size("latent")
    direct = paired(w_dec.shape[1], peers, inputs.shape[1], inputs.shape[2])
    if direct:
        whole = gather(inputs[0], peers)
        positive, act, partial = forward(src, whole, w_enc[0], b_enc, w_dec[0], bf16)
        errors, grad_bdec = exchange(partial, targets[0], b_dec, peers)
    else:
        whole = lax.all_gather(inputs[0], "latent", axis=0, tiled=True)
        positive, act, partial = forward(src, whole, w_enc[0], b_enc, w_dec[0], f32)
        spread = lax.psum_scatter(partial, "layer", scatter_dimension=0, tiled=True)
        recon = lax.psum_scatter(spread, "latent", scatter_dimension=1, tiled=True)
        error = recon[0] + b_dec[0] - targets[0].astype(f32)
        err_low = error.astype(bf16)[None]
        stacked = lax.all_gather(err_low, "latent", axis=1, tiled=True)
        errors = lax.all_gather(stacked, "layer", axis=0, tiled=True)
        grad_bdec = lax.psum(jnp.sum(error, axis=0), "latent")[None, :]
    grad_enc, grad_benc, grad_dec = backward(src, whole, positive, act, errors, w_dec[0])
    return (grad_enc[None], grad_benc, grad_dec[None], grad_bdec)


def solution(mesh):
    placed = (
        P("layer", "latent", None),
        P("layer", "latent", None),
        P("layer", None, "latent"),
        P("layer", "latent"),
        P("layer", None, "latent", None),
        P("layer", None),
    )
    return jax.shard_map(
        local,
        mesh=mesh,
        in_specs=placed,
        out_specs=(
            P("layer", None, "latent"),
            P("layer", "latent"),
            P("layer", None, "latent", None),
            P("layer", None),
        ),
        check_vma=False,
    )
```

```python
import functools

import jax
import jax.numpy as jnp
from jax import lax
from jax.experimental import pallas as pl
from jax.experimental.pallas import tpu as pltpu
from jax.sharding import PartitionSpec as P

penalty = 0.5
eps = 1e-06
f32 = jnp.float32
bf16 = jnp.bfloat16
VMEM_LIMIT = 60 * 1024 * 1024


def forward_kernel(src, *refs):
    forward_body(src[0], *refs)


def forward_body(layer, whole, w_enc, b_enc, w_dec, positive, act, partial, total):
    step = pl.program_id(0)
    depth = w_dec.shape[0]
    features = w_dec.shape[2]
    cols = min(features, 1024)

    @pl.when(step == 0)
    def _():
        total[...] = jnp.zeros_like(total)

    pre = jnp.dot(whole[...], w_enc[...], preferred_element_type=f32) + b_enc[...]
    pos = jnp.maximum(pre, 0.0)
    positive[...] = pos
    act[...] = (pos * pos).astype(bf16)
    for t in range(depth):

        @pl.when(t >= layer)
        def _():
            for c in range(0, features, cols):
                total[t, :, c : c + cols] += jnp.dot(
                    act[...], w_dec[t, :, c : c + cols], preferred_element_type=f32
                )

    @pl.when(step == pl.num_programs(0) - 1)
    def _():
        for t in range(depth):
            partial[t] = total[t].astype(partial.dtype)


def forward(src, whole, w_enc, b_enc, w_dec, out_dtype):
    tokens, features = whole.shape
    depth, latents, _ = w_dec.shape
    block = min(latents, 256)
    return pl.pallas_call(
        forward_kernel,
        grid_spec=pltpu.PrefetchScalarGridSpec(
            num_scalar_prefetch=1,
            grid=(latents // block,),
            in_specs=[
                pl.BlockSpec((tokens, features), lambda i, s: (0, 0), pipeline_mode=pl.Buffered(1)),
                pl.BlockSpec((features, block), lambda i, s: (0, i)),
                pl.BlockSpec((1, block), lambda i, s: (0, i)),
                pl.BlockSpec((depth, block, features), lambda i, s: (0, i, 0)),
            ],
            out_specs=[
                pl.BlockSpec((tokens, block), lambda i, s: (0, i)),
                pl.BlockSpec((tokens, block), lambda i, s: (0, i)),
                pl.BlockSpec((depth, tokens, features), lambda i, s: (0, 0, 0), pipeline_mode=pl.Buffered(1)),
            ],
            scratch_shapes=[pltpu.VMEM((depth, tokens, features), f32)],
        ),
        out_shape=[
            jax.ShapeDtypeStruct((tokens, latents), f32),
            jax.ShapeDtypeStruct((tokens, latents), bf16),
            jax.ShapeDtypeStruct((depth, tokens, features), out_dtype),
        ],
        compiler_params=pltpu.CompilerParams(
            dimension_semantics=("arbitrary",), vmem_limit_bytes=VMEM_LIMIT
        ),
    )(src, whole, w_enc, b_enc, w_dec)


def backward_kernel(
    src, whole, positive, act, errors, w_dec, grad_enc, grad_benc, grad_dec, flipped, back, squares
):
    depth, block, features = w_dec.shape
    cols = min(features, 512)
    lanes = 128

    @pl.when(pl.program_id(0) == 0)
    def _():
        flipped[...] = whole[...].T

    back[...] = jnp.zeros_like(back)
    squares[...] = jnp.zeros_like(squares)
    for t in range(depth):

        @pl.when(t >= src[0])
        def _():
            back[...] += lax.dot_general(
                errors[t], w_dec[t], (((1,), (1,)), ((), ())), preferred_element_type=f32
            )
            partial = squares[...]
            for c in range(0, features, lanes):
                wide = w_dec[t, :, c : c + lanes].astype(f32)
                partial = partial + wide * wide
            squares[...] = partial

    sums = squares[...]
    norm_row = jnp.sqrt(jnp.sum(sums.T, axis=0, keepdims=True) + eps)
    norm_col = jnp.sqrt(jnp.sum(sums, axis=1, keepdims=True) + eps)
    d_pre = (back[...] + penalty * norm_row) * 2.0 * positive[...]
    grad_benc[...] = jnp.sum(d_pre, axis=0, keepdims=True)
    grad_enc[...] = jnp.dot(
        flipped[...], d_pre.astype(bf16), preferred_element_type=f32
    ).astype(bf16)
    turned = act[...].astype(f32).T
    scale = penalty * jnp.sum(turned, axis=1, keepdims=True) / norm_col
    turned = turned.astype(bf16)
    for t in range(depth):

        @pl.when(t >= src[0])
        def _():
            for c in range(0, features, cols):
                mse = jnp.dot(turned, errors[t, :, c : c + cols], preferred_element_type=f32)
                grad_dec[t, :, c : c + cols] = (
                    mse + scale * w_dec[t, :, c : c + cols].astype(f32)
                ).astype(bf16)

        @pl.when(t < src[0])
        def _():
            grad_dec[t] = jnp.zeros_like(grad_dec[t])


def backward(src, whole, positive, act, errors, w_dec):
    tokens, features = whole.shape
    depth, latents, _ = w_dec.shape
    block = min(latents, 256)
    return pl.pallas_call(
        backward_kernel,
        grid_spec=pltpu.PrefetchScalarGridSpec(
            num_scalar_prefetch=1,
            grid=(latents // block,),
            in_specs=[
                pl.BlockSpec((tokens, features), lambda i, s: (0, 0), pipeline_mode=pl.Buffered(1)),
                pl.BlockSpec((tokens, block), lambda i, s: (0, i)),
                pl.BlockSpec((tokens, block), lambda i, s: (0, i)),
                pl.BlockSpec((depth, tokens, features), lambda i, s: (0, 0, 0), pipeline_mode=pl.Buffered(1)),
                pl.BlockSpec((depth, block, features), lambda i, s: (0, i, 0)),
            ],
            out_specs=[
                pl.BlockSpec((features, block), lambda i, s: (0, i)),
                pl.BlockSpec((1, block), lambda i, s: (0, i)),
                pl.BlockSpec((depth, block, features), lambda i, s: (0, i, 0)),
            ],
            scratch_shapes=[
                pltpu.VMEM((features, tokens), bf16),
                pltpu.VMEM((tokens, block), f32),
                pltpu.VMEM((block, 128), f32),
            ],
        ),
        out_shape=[
            jax.ShapeDtypeStruct((features, latents), bf16),
            jax.ShapeDtypeStruct((1, latents), f32),
            jax.ShapeDtypeStruct((depth, latents, features), bf16),
        ],
        compiler_params=pltpu.CompilerParams(
            dimension_semantics=("arbitrary",), vmem_limit_bytes=VMEM_LIMIT
        ),
    )(src, whole, positive, act, errors, w_dec)


MESH = pl.DeviceIdType.MESH


def place():
    layer, latent = lax.axis_index("layer"), lax.axis_index("latent")
    return layer // 2, lax.rem(layer, 2), latent // 2, lax.rem(latent, 2)


def remote(src, dst, send, recv, target):
    return pltpu.make_async_remote_copy(
        src_ref=src, dst_ref=dst, send_sem=send, recv_sem=recv, device_id=target, device_id_type=MESH
    )


def greet(partners):
    barrier = pltpu.get_barrier_semaphore()
    for partner in partners:
        pl.semaphore_signal(barrier, inc=1, device_id=partner, device_id_type=MESH)
    pl.semaphore_wait(barrier, len(partners))


def gather_kernel(rows, own, whole, send_z, recv_z, send_x, recv_x):
    y, c, z, x = place()
    layer = 2 * y + c
    mine = 2 * z + x
    beside = (layer, 2 * z + 1 - x)
    along = [(layer, 2 * lax.rem(z + d, rows) + x) for d in range(rows)]
    greet([beside] + along[1:])
    sent = []
    order = sorted(range(1, rows), key=lambda d: abs(2 * d - rows))
    for d in order:
        copy = remote(own, whole.at[mine], send_z.at[d], recv_z.at[d], along[d])
        copy.start()
        sent.append(copy)
    first = remote(own, whole.at[mine], send_x.at[0], recv_x.at[0], beside)
    first.start()
    whole[mine] = own[...]
    across = [first]
    for d in range(1, rows):
        start = 2 * lax.rem(z + rows - d, rows) + x
        remote(own, whole.at[start], send_z.at[d], recv_z.at[d], along[d]).wait_recv()
        copy = remote(whole.at[start], whole.at[start], send_x.at[d], recv_x.at[d], beside)
        copy.start()
        across.append(copy)
    for copy in sent:
        copy.wait_send()
    for copy in across:
        copy.wait()


def joined_kernel(
    rows, own, w_enc, b_enc, w_dec, positive, act, partial, everything,
    total, landing, send_z, recv_z, send_x, recv_x,
):
    @pl.when(pl.program_id(0) == 0)
    def _():
        gather_kernel(rows, own, landing, send_z, recv_z, send_x, recv_x)
        for i in range(2 * rows):
            chunk = own.shape[0]
            everything[i * chunk : (i + 1) * chunk, :] = landing[i]

    forward_body(
        lax.axis_index("layer"), everything, w_enc, b_enc, w_dec, positive, act, partial, total
    )


def joined(own, w_enc, b_enc, w_dec, peers):
    chunk, features = own.shape
    tokens = chunk * peers
    depth, latents, _ = w_dec.shape
    block = min(latents, 256)
    rows = peers // 2
    dma = pltpu.SemaphoreType.DMA((rows,))
    return pl.pallas_call(
        functools.partial(joined_kernel, rows),
        grid_spec=pltpu.PrefetchScalarGridSpec(
            num_scalar_prefetch=0,
            grid=(latents // block,),
            in_specs=[
                pl.BlockSpec((chunk, features), lambda i: (0, 0), pipeline_mode=pl.Buffered(1)),
                pl.BlockSpec((features, block), lambda i: (0, i)),
                pl.BlockSpec((1, block), lambda i: (0, i)),
                pl.BlockSpec((depth, block, features), lambda i: (0, i, 0)),
            ],
            out_specs=[
                pl.BlockSpec((tokens, block), lambda i: (0, i)),
                pl.BlockSpec((tokens, block), lambda i: (0, i)),
                pl.BlockSpec((depth, tokens, features), lambda i: (0, 0, 0), pipeline_mode=pl.Buffered(1)),
                pl.BlockSpec((tokens, features), lambda i: (0, 0), pipeline_mode=pl.Buffered(1)),
            ],
            scratch_shapes=[
                pltpu.VMEM((depth, tokens, features), f32),
                pltpu.VMEM((peers, chunk, features), bf16),
            ] + [dma] * 4,
        ),
        out_shape=[
            jax.ShapeDtypeStruct((tokens, latents), f32),
            jax.ShapeDtypeStruct((tokens, latents), bf16),
            jax.ShapeDtypeStruct((depth, tokens, features), bf16),
            jax.ShapeDtypeStruct((tokens, features), bf16),
        ],
        compiler_params=pltpu.CompilerParams(
            dimension_semantics=("arbitrary",), vmem_limit_bytes=VMEM_LIMIT,
            collective_id=0, has_side_effects=True,
        ),
    )(own, w_enc, b_enc, w_dec)


def exchange_kernel(
    rows, part, targets, b_dec, errors, grad_bdec,
    core_in, out_x, in_x, out_z, in_z, own, out_y, in_y, biases,
    send_c, recv_c, send_x, recv_x, send_z, recv_z, send_y, recv_y,
    send_ez, recv_ez, send_ex, recv_ex, send_ec, recv_ec, send_b, recv_b,
):
    y, c, z, x = place()
    layer = 2 * y + c
    mine = 2 * z + x
    peers = 2 * rows
    core = (2 * y + 1 - c, mine)
    beside = (layer, 2 * z + 1 - x)
    across = (2 * (1 - y) + c, mine)
    along = [(layer, 2 * lax.rem(z + d, rows) + x) for d in range(rows)]
    everyone = [(layer, lax.rem(mine + o, peers)) for o in range(peers)]
    greet([core, across] + everyone[1:])
    bottom, top = y == 0, y == 1

    def only(k, body):
        if k == 1:
            body()
        else:
            pl.when(bottom)(body)

    def pair(d):
        return pl.ds(2 * lax.rem(z + d, rows), 2)

    def core_copy(k, d):
        return remote(
            part.at[1 - c + 2 * k, pair(d)], core_in.at[k, pair(d)], send_c.at[k, d], recv_c.at[k, d], core
        )

    def x_copy(k, d):
        return remote(out_x.at[k, d], in_x.at[k, d], send_x.at[k, d], recv_x.at[k, d], beside)

    def z_copy(k, d):
        return remote(out_z.at[k, d], in_z.at[k, d], send_z.at[k, d], recv_z.at[k, d], along[d])

    def both(k, at):
        return part[c + 2 * k, at].astype(f32) + core_in[k, at].astype(f32)

    def first(k, d):
        def body():
            core_copy(k, d).wait_recv()
            at = 2 * lax.rem(z + d, rows) + 1 - x
            out_x[k, d] = both(k, at).astype(bf16)
            x_copy(k, d).start()

        only(k, body)

    def second(k, d):
        def body():
            x_copy(k, d).wait_recv()
            at = 2 * lax.rem(z + d, rows) + x
            value = both(k, at) + in_x[k, d].astype(f32)
            if d == 0:
                own[k] = value
            else:
                out_z[k, d] = value.astype(bf16)
                z_copy(k, d).start()

        only(k, body)

    def collect(k):
        value = own[k]
        for d in range(1, rows):
            z_copy(k, d).wait_recv()
            value = value + in_z[k, d].astype(f32)
        return value

    def bias_copy(o):
        return remote(biases.at[mine], biases.at[mine], send_b.at[o], recv_b.at[o], everyone[o])

    def settle(value, k):
        error = value + b_dec[...] - targets[...].astype(f32)
        errors[c + 2 * k, mine] = error.astype(bf16)
        total = jnp.sum(error, axis=0, keepdims=True)
        width = total.shape[1] // 8
        for i in range(8):
            biases[mine, i : i + 1, :] = total[:, i * width : (i + 1) * width]

    up = remote(out_y, in_y, send_y.at[0], recv_y.at[0], across)
    high = errors.at[c + 2, mine]
    down = remote(high, high, send_y.at[1], recv_y.at[1], across)

    def spread_z(k, d):
        ref = errors.at[c + 2 * k, mine]
        return remote(ref, ref, send_ez.at[k, d], recv_ez.at[k, d], along[d])

    def spread_x(k, d):
        ref = errors.at[c + 2 * k, 2 * lax.rem(z + rows - d, rows) + x]
        return remote(ref, ref, send_ex.at[k, d], recv_ex.at[k, d], beside)

    def spread_c(k, d, side):
        ref = errors.at[side + 2 * k, pl.ds(2 * lax.rem(z + rows - d, rows), 2)]
        return remote(ref, ref, send_ec.at[k, d], recv_ec.at[k, d], core)

    def launch(k):
        for d in list(range(rows // 2, 0, -1)) + list(range(rows // 2 + 1, rows)):
            spread_z(k, d).start()
        spread_x(k, 0).start()

    units = [(k, d) for k in (1, 0) for d in list(range(1, rows)) + [0]]
    for k, d in units:
        only(k, core_copy(k, d).start)
    lag = 2
    for i in range(len(units) + lag):
        if i < len(units):
            first(*units[i])
        if i >= lag:
            second(*units[i - lag])
        if i == len(units) - 1:

            @pl.when(bottom)
            def _():
                out_y[...] = collect(1).astype(bf16)
                up.start()

            @pl.when(top)
            def _():
                value = collect(1)
                up.wait_recv()
                settle(value + in_y[...].astype(f32), 1)
                down.start()
                launch(1)

    @pl.when(bottom)
    def _():
        settle(collect(0), 0)
        launch(0)
        down.wait_recv()
        launch(1)

    for o in range(1, peers):
        bias_copy(o).start()

    for k in (0, 1):

        def relay(k=k):
            for d in range(1, rows):
                spread_z(k, d).wait_recv()
                spread_x(k, d).start()

        only(k, relay)

    forwards = {1: jnp.logical_or(bottom, c == 1), 0: jnp.logical_and(bottom, c == 1)}
    receives = {1: jnp.logical_or(bottom, c == 0), 0: jnp.logical_and(bottom, c == 0)}
    for k in (0, 1):

        def finish(k=k):
            for d in range(rows):
                spread_x(k, d).wait_recv()

                @pl.when(forwards[k])
                def _():
                    spread_c(k, d, c).start()

        only(k, finish)

    for o in range(1, peers):
        bias_copy(o).wait()
    total = biases[0]
    for i in range(1, peers):
        total = total + biases[i]
    width = total.shape[1]
    for i in range(8):
        grad_bdec[:, i * width : (i + 1) * width] = total[i : i + 1, :]

    for k in (0, 1):

        @pl.when(receives[k])
        def _():
            for d in range(rows):
                spread_c(k, d, 1 - c).wait_recv()

        @pl.when(forwards[k])
        def _():
            for d in range(rows):
                spread_c(k, d, c).wait_send()

        def drain(k=k):
            for d in range(rows):
                core_copy(k, d).wait_send()
                x_copy(k, d).wait_send()
                spread_x(k, d).wait_send()
                if d:
                    z_copy(k, d).wait_send()
                    spread_z(k, d).wait_send()

        only(k, drain)

    pl.when(bottom)(up.wait_send)
    pl.when(top)(down.wait_send)


def exchange(partial, targets, b_dec, peers):
    depth, tokens, features = partial.shape
    rows = peers // 2
    chunk = tokens // peers
    slots = pltpu.VMEM((2, rows, chunk, features), bf16)
    dma = pltpu.SemaphoreType.DMA((2, rows))
    flat = pltpu.SemaphoreType.DMA((peers,))
    errors, grad_bdec = pl.pallas_call(
        functools.partial(exchange_kernel, rows),
        out_shape=[
            jax.ShapeDtypeStruct((depth, peers, chunk, features), bf16),
            jax.ShapeDtypeStruct((1, features), f32),
        ],
        in_specs=[pl.BlockSpec(memory_space=pltpu.VMEM)] * 3,
        out_specs=[pl.BlockSpec(memory_space=pltpu.VMEM)] * 2,
        scratch_shapes=[
            pltpu.VMEM((2, peers, chunk, features), bf16),
            slots, slots, slots, slots,
            pltpu.VMEM((2, chunk, features), f32),
            pltpu.VMEM((chunk, features), bf16),
            pltpu.VMEM((chunk, features), bf16),
            pltpu.VMEM((peers, 8, features // 8), f32),
        ] + [dma] * 6 + [pltpu.SemaphoreType.DMA((2,))] * 2 + [dma] * 6 + [flat] * 2,
        compiler_params=pltpu.CompilerParams(
            collective_id=1, has_side_effects=True, vmem_limit_bytes=VMEM_LIMIT
        ),
    )(partial.reshape(depth, peers, chunk, features), targets, b_dec)
    return errors.reshape(depth, tokens, features), grad_bdec


def paired(depth, peers, chunk, features):
    layers = lax.axis_size("layer")
    return layers == depth == 4 and peers % 2 == 0 and chunk % 16 == 0 and features % 1024 == 0


def local(inputs, targets, w_enc, b_enc, w_dec, b_dec):
    src = lax.axis_index("layer").astype(jnp.int32)[None]
    peers = lax.axis_size("latent")
    direct = paired(w_dec.shape[1], peers, inputs.shape[1], inputs.shape[2])
    if direct:
        positive, act, partial, whole = joined(inputs[0], w_enc[0], b_enc, w_dec[0], peers)
        errors, grad_bdec = exchange(partial, targets[0], b_dec, peers)
    else:
        whole = lax.all_gather(inputs[0], "latent", axis=0, tiled=True)
        positive, act, partial = forward(src, whole, w_enc[0], b_enc, w_dec[0], f32)
        spread = lax.psum_scatter(partial, "layer", scatter_dimension=0, tiled=True)
        recon = lax.psum_scatter(spread, "latent", scatter_dimension=1, tiled=True)
        error = recon[0] + b_dec[0] - targets[0].astype(f32)
        err_low = error.astype(bf16)[None]
        stacked = lax.all_gather(err_low, "latent", axis=1, tiled=True)
        errors = lax.all_gather(stacked, "layer", axis=0, tiled=True)
        grad_bdec = lax.psum(jnp.sum(error, axis=0), "latent")[None, :]
    grad_enc, grad_benc, grad_dec = backward(src, whole, positive, act, errors, w_dec[0])
    return (grad_enc[None], grad_benc, grad_dec[None], grad_bdec)


def solution(mesh):
    placed = (
        P("layer", "latent", None),
        P("layer", "latent", None),
        P("layer", None, "latent"),
        P("layer", "latent"),
        P("layer", None, "latent", None),
        P("layer", None),
    )
    return jax.shard_map(
        local,
        mesh=mesh,
        in_specs=placed,
        out_specs=(
            P("layer", None, "latent"),
            P("layer", "latent"),
            P("layer", None, "latent", None),
            P("layer", None),
        ),
        check_vma=False,
    )
```

```python
import functools

import jax
import jax.numpy as jnp
from jax import lax
from jax.experimental import pallas as pl
from jax.experimental.pallas import tpu as pltpu
from jax.sharding import PartitionSpec as P

penalty = 0.5
eps = 1e-06
f32 = jnp.float32
bf16 = jnp.bfloat16
VMEM_LIMIT = 60 * 1024 * 1024


def forward_kernel(src, *refs):
    forward_body(src[0], *refs)


def forward_body(layer, whole, w_enc, b_enc, w_dec, positive, act, partial, total):
    step = pl.program_id(0)
    depth = w_dec.shape[0]
    features = w_dec.shape[2]
    cols = min(features, 1024)

    last = pl.num_programs(0) - 1
    pre = jnp.dot(whole[...], w_enc[...], preferred_element_type=f32) + b_enc[...]
    pos = jnp.maximum(pre, 0.0)
    positive[...] = pos
    act[...] = (pos * pos).astype(bf16)

    def term(t, c):
        return jnp.dot(act[...], w_dec[t, :, c : c + cols], preferred_element_type=f32)

    for t in range(depth):
        used = t >= layer

        @pl.when(used & (step == 0))
        def _():
            for c in range(0, features, cols):
                total[t, :, c : c + cols] = term(t, c)

        @pl.when(used & (step > 0) & (step < last))
        def _():
            for c in range(0, features, cols):
                total[t, :, c : c + cols] += term(t, c)

        @pl.when(used & (step > 0) & (step == last))
        def _():
            for c in range(0, features, cols):
                partial[t, :, c : c + cols] = (total[t, :, c : c + cols] + term(t, c)).astype(partial.dtype)

        @pl.when(used & (step == 0) & (step == last))
        def _():
            partial[t] = total[t].astype(partial.dtype)

        @pl.when((t < layer) & (step == last))
        def _():
            partial[t] = jnp.zeros_like(partial[t])


def forward(src, whole, w_enc, b_enc, w_dec, out_dtype):
    tokens, features = whole.shape
    depth, latents, _ = w_dec.shape
    block = min(latents, 256)
    return pl.pallas_call(
        forward_kernel,
        grid_spec=pltpu.PrefetchScalarGridSpec(
            num_scalar_prefetch=1,
            grid=(latents // block,),
            in_specs=[
                pl.BlockSpec((tokens, features), lambda i, s: (0, 0), pipeline_mode=pl.Buffered(1)),
                pl.BlockSpec((features, block), lambda i, s: (0, i)),
                pl.BlockSpec((1, block), lambda i, s: (0, i)),
                pl.BlockSpec((depth, block, features), lambda i, s: (0, i, 0)),
            ],
            out_specs=[
                pl.BlockSpec((tokens, block), lambda i, s: (0, i)),
                pl.BlockSpec((tokens, block), lambda i, s: (0, i)),
                pl.BlockSpec((depth, tokens, features), lambda i, s: (0, 0, 0), pipeline_mode=pl.Buffered(1)),
            ],
            scratch_shapes=[pltpu.VMEM((depth, tokens, features), f32)],
        ),
        out_shape=[
            jax.ShapeDtypeStruct((tokens, latents), f32),
            jax.ShapeDtypeStruct((tokens, latents), bf16),
            jax.ShapeDtypeStruct((depth, tokens, features), out_dtype),
        ],
        compiler_params=pltpu.CompilerParams(
            dimension_semantics=("arbitrary",), vmem_limit_bytes=VMEM_LIMIT
        ),
    )(src, whole, w_enc, b_enc, w_dec)


def backward_kernel(
    src, whole, positive, act, errors, w_dec, grad_enc, grad_benc, grad_dec, flipped, back, squares
):
    depth, block, features = w_dec.shape
    cols = min(features, 512)
    lanes = 128

    @pl.when(pl.program_id(0) == 0)
    def _():
        flipped[...] = whole[...].T

    back[...] = jnp.zeros_like(back)
    squares[...] = jnp.zeros_like(squares)
    for t in range(depth):

        @pl.when(t >= src[0])
        def _():
            back[...] += lax.dot_general(
                errors[t], w_dec[t], (((1,), (1,)), ((), ())), preferred_element_type=f32
            )
            partial = squares[...]
            for c in range(0, features, lanes):
                wide = w_dec[t, :, c : c + lanes].astype(f32)
                partial = partial + wide * wide
            squares[...] = partial

    sums = squares[...]
    norm_row = jnp.sqrt(jnp.sum(sums.T, axis=0, keepdims=True) + eps)
    norm_col = jnp.sqrt(jnp.sum(sums, axis=1, keepdims=True) + eps)
    d_pre = (back[...] + penalty * norm_row) * 2.0 * positive[...]
    grad_benc[...] = jnp.sum(d_pre, axis=0, keepdims=True)
    grad_enc[...] = jnp.dot(
        flipped[...], d_pre.astype(bf16), preferred_element_type=f32
    ).astype(bf16)
    turned = act[...].astype(f32).T
    scale = penalty * jnp.sum(turned, axis=1, keepdims=True) / norm_col
    turned = turned.astype(bf16)
    for t in range(depth):

        @pl.when(t >= src[0])
        def _():
            for c in range(0, features, cols):
                mse = jnp.dot(turned, errors[t, :, c : c + cols], preferred_element_type=f32)
                grad_dec[t, :, c : c + cols] = (
                    mse + scale * w_dec[t, :, c : c + cols].astype(f32)
                ).astype(bf16)

        @pl.when(t < src[0])
        def _():
            grad_dec[t] = jnp.zeros_like(grad_dec[t])


def backward(src, whole, positive, act, errors, w_dec):
    tokens, features = whole.shape
    depth, latents, _ = w_dec.shape
    block = min(latents, 256)
    return pl.pallas_call(
        backward_kernel,
        grid_spec=pltpu.PrefetchScalarGridSpec(
            num_scalar_prefetch=1,
            grid=(latents // block,),
            in_specs=[
                pl.BlockSpec((tokens, features), lambda i, s: (0, 0), pipeline_mode=pl.Buffered(1)),
                pl.BlockSpec((tokens, block), lambda i, s: (0, i)),
                pl.BlockSpec((tokens, block), lambda i, s: (0, i)),
                pl.BlockSpec((depth, tokens, features), lambda i, s: (0, 0, 0), pipeline_mode=pl.Buffered(1)),
                pl.BlockSpec((depth, block, features), lambda i, s: (0, i, 0)),
            ],
            out_specs=[
                pl.BlockSpec((features, block), lambda i, s: (0, i)),
                pl.BlockSpec((1, block), lambda i, s: (0, i)),
                pl.BlockSpec((depth, block, features), lambda i, s: (0, i, 0)),
            ],
            scratch_shapes=[
                pltpu.VMEM((features, tokens), bf16),
                pltpu.VMEM((tokens, block), f32),
                pltpu.VMEM((block, 128), f32),
            ],
        ),
        out_shape=[
            jax.ShapeDtypeStruct((features, latents), bf16),
            jax.ShapeDtypeStruct((1, latents), f32),
            jax.ShapeDtypeStruct((depth, latents, features), bf16),
        ],
        compiler_params=pltpu.CompilerParams(
            dimension_semantics=("arbitrary",), vmem_limit_bytes=VMEM_LIMIT
        ),
    )(src, whole, positive, act, errors, w_dec)


MESH = pl.DeviceIdType.MESH


def place():
    layer, latent = lax.axis_index("layer"), lax.axis_index("latent")
    return layer // 2, lax.rem(layer, 2), latent // 2, lax.rem(latent, 2)


def remote(src, dst, send, recv, target):
    return pltpu.make_async_remote_copy(
        src_ref=src, dst_ref=dst, send_sem=send, recv_sem=recv, device_id=target, device_id_type=MESH
    )


def greet(partners):
    barrier = pltpu.get_barrier_semaphore()
    for partner in partners:
        pl.semaphore_signal(barrier, inc=1, device_id=partner, device_id_type=MESH)
    pl.semaphore_wait(barrier, len(partners))


def gather_kernel(rows, own, whole, send_z, recv_z, send_x, recv_x):
    y, c, z, x = place()
    layer = 2 * y + c
    mine = 2 * z + x
    beside = (layer, 2 * z + 1 - x)
    along = [(layer, 2 * lax.rem(z + d, rows) + x) for d in range(rows)]
    greet([beside] + along[1:])
    sent = []
    order = sorted(range(1, rows), key=lambda d: abs(2 * d - rows))
    for d in order:
        copy = remote(own, whole.at[mine], send_z.at[d], recv_z.at[d], along[d])
        copy.start()
        sent.append(copy)
    first = remote(own, whole.at[mine], send_x.at[0], recv_x.at[0], beside)
    first.start()
    whole[mine] = own[...]
    across = [first]
    for d in range(1, rows):
        start = 2 * lax.rem(z + rows - d, rows) + x
        remote(own, whole.at[start], send_z.at[d], recv_z.at[d], along[d]).wait_recv()
        copy = remote(whole.at[start], whole.at[start], send_x.at[d], recv_x.at[d], beside)
        copy.start()
        across.append(copy)
    for copy in sent:
        copy.wait_send()
    for copy in across:
        copy.wait()


def joined_kernel(
    rows, own, w_enc, b_enc, w_dec, positive, act, partial, everything,
    total, landing, send_z, recv_z, send_x, recv_x,
):
    @pl.when(pl.program_id(0) == 0)
    def _():
        gather_kernel(rows, own, landing, send_z, recv_z, send_x, recv_x)
        for i in range(2 * rows):
            chunk = own.shape[0]
            everything[i * chunk : (i + 1) * chunk, :] = landing[i]

    forward_body(
        lax.axis_index("layer"), everything, w_enc, b_enc, w_dec, positive, act, partial, total
    )


def joined(own, w_enc, b_enc, w_dec, peers):
    chunk, features = own.shape
    tokens = chunk * peers
    depth, latents, _ = w_dec.shape
    block = min(latents, 256)
    rows = peers // 2
    dma = pltpu.SemaphoreType.DMA((rows,))
    return pl.pallas_call(
        functools.partial(joined_kernel, rows),
        grid_spec=pltpu.PrefetchScalarGridSpec(
            num_scalar_prefetch=0,
            grid=(latents // block,),
            in_specs=[
                pl.BlockSpec((chunk, features), lambda i: (0, 0), pipeline_mode=pl.Buffered(1)),
                pl.BlockSpec((features, block), lambda i: (0, i)),
                pl.BlockSpec((1, block), lambda i: (0, i)),
                pl.BlockSpec((depth, block, features), lambda i: (0, i, 0)),
            ],
            out_specs=[
                pl.BlockSpec((tokens, block), lambda i: (0, i)),
                pl.BlockSpec((tokens, block), lambda i: (0, i)),
                pl.BlockSpec((depth, tokens, features), lambda i: (0, 0, 0), pipeline_mode=pl.Buffered(1)),
                pl.BlockSpec((tokens, features), lambda i: (0, 0), pipeline_mode=pl.Buffered(1)),
            ],
            scratch_shapes=[
                pltpu.VMEM((depth, tokens, features), f32),
                pltpu.VMEM((peers, chunk, features), bf16),
            ] + [dma] * 4,
        ),
        out_shape=[
            jax.ShapeDtypeStruct((tokens, latents), f32),
            jax.ShapeDtypeStruct((tokens, latents), bf16),
            jax.ShapeDtypeStruct((depth, tokens, features), bf16),
            jax.ShapeDtypeStruct((tokens, features), bf16),
        ],
        compiler_params=pltpu.CompilerParams(
            dimension_semantics=("arbitrary",), vmem_limit_bytes=VMEM_LIMIT,
            collective_id=0, has_side_effects=True,
        ),
    )(own, w_enc, b_enc, w_dec)


def exchange_kernel(
    rows, part, targets, b_dec, errors, grad_bdec,
    core_in, out_x, in_x, out_z, in_z, own, out_y, in_y, biases,
    send_c, recv_c, send_x, recv_x, send_z, recv_z, send_y, recv_y,
    send_ez, recv_ez, send_ex, recv_ex, send_ec, recv_ec, send_b, recv_b,
):
    y, c, z, x = place()
    layer = 2 * y + c
    mine = 2 * z + x
    peers = 2 * rows
    core = (2 * y + 1 - c, mine)
    beside = (layer, 2 * z + 1 - x)
    across = (2 * (1 - y) + c, mine)
    along = [(layer, 2 * lax.rem(z + d, rows) + x) for d in range(rows)]
    everyone = [(layer, lax.rem(mine + o, peers)) for o in range(peers)]
    greet([core, across] + everyone[1:])
    bottom, top = y == 0, y == 1

    def only(k, body):
        if k == 1:
            body()
        else:
            pl.when(bottom)(body)

    def pair(d):
        return pl.ds(2 * lax.rem(z + d, rows), 2)

    def core_copy(k, d):
        return remote(
            part.at[1 - c + 2 * k, pair(d)], core_in.at[k, pair(d)], send_c.at[k, d], recv_c.at[k, d], core
        )

    def x_copy(k, d):
        return remote(out_x.at[k, d], in_x.at[k, d], send_x.at[k, d], recv_x.at[k, d], beside)

    def z_copy(k, d):
        return remote(out_z.at[k, d], in_z.at[k, d], send_z.at[k, d], recv_z.at[k, d], along[d])

    def both(k, at):
        return part[c + 2 * k, at].astype(f32) + core_in[k, at].astype(f32)

    def first(k, d):
        def body():
            core_copy(k, d).wait_recv()
            at = 2 * lax.rem(z + d, rows) + 1 - x
            out_x[k, d] = both(k, at).astype(bf16)
            x_copy(k, d).start()

        only(k, body)

    def second(k, d):
        def body():
            x_copy(k, d).wait_recv()
            at = 2 * lax.rem(z + d, rows) + x
            value = both(k, at) + in_x[k, d].astype(f32)
            if d == 0:
                own[k] = value
            else:
                out_z[k, d] = value.astype(bf16)
                z_copy(k, d).start()

        only(k, body)

    def collect(k):
        value = own[k]
        for d in range(1, rows):
            z_copy(k, d).wait_recv()
            value = value + in_z[k, d].astype(f32)
        return value

    def bias_copy(o):
        return remote(biases.at[mine], biases.at[mine], send_b.at[o], recv_b.at[o], everyone[o])

    def settle(value, k):
        error = value + b_dec[...] - targets[...].astype(f32)
        errors[c + 2 * k, mine] = error.astype(bf16)
        total = jnp.sum(error, axis=0, keepdims=True)
        width = total.shape[1] // 8
        for i in range(8):
            biases[mine, i : i + 1, :] = total[:, i * width : (i + 1) * width]

    up = remote(out_y, in_y, send_y.at[0], recv_y.at[0], across)
    high = errors.at[c + 2, mine]
    down = remote(high, high, send_y.at[1], recv_y.at[1], across)

    def spread_z(k, d):
        ref = errors.at[c + 2 * k, mine]
        return remote(ref, ref, send_ez.at[k, d], recv_ez.at[k, d], along[d])

    def spread_x(k, d):
        ref = errors.at[c + 2 * k, 2 * lax.rem(z + rows - d, rows) + x]
        return remote(ref, ref, send_ex.at[k, d], recv_ex.at[k, d], beside)

    def spread_c(k, d, side):
        ref = errors.at[side + 2 * k, pl.ds(2 * lax.rem(z + rows - d, rows), 2)]
        return remote(ref, ref, send_ec.at[k, d], recv_ec.at[k, d], core)

    def launch(k):
        for d in list(range(rows // 2, 0, -1)) + list(range(rows // 2 + 1, rows)):
            spread_z(k, d).start()
        spread_x(k, 0).start()

    units = [(k, d) for k in (1, 0) for d in list(range(1, rows)) + [0]]
    for k, d in units:
        only(k, core_copy(k, d).start)
    lag = 2
    for i in range(len(units) + lag):
        if i < len(units):
            first(*units[i])
        if i >= lag:
            second(*units[i - lag])
        if i == len(units) - 1:

            @pl.when(bottom)
            def _():
                out_y[...] = collect(1).astype(bf16)
                up.start()

            @pl.when(top)
            def _():
                value = collect(1)
                up.wait_recv()
                settle(value + in_y[...].astype(f32), 1)
                down.start()
                launch(1)

    @pl.when(bottom)
    def _():
        settle(collect(0), 0)
        launch(0)
        down.wait_recv()
        launch(1)

    for o in range(1, peers):
        bias_copy(o).start()

    for k in (0, 1):

        def relay(k=k):
            for d in range(1, rows):
                spread_z(k, d).wait_recv()
                spread_x(k, d).start()

        only(k, relay)

    forwards = {1: jnp.logical_or(bottom, c == 1), 0: jnp.logical_and(bottom, c == 1)}
    receives = {1: jnp.logical_or(bottom, c == 0), 0: jnp.logical_and(bottom, c == 0)}
    for k in (0, 1):

        def finish(k=k):
            for d in range(rows):
                spread_x(k, d).wait_recv()

                @pl.when(forwards[k])
                def _():
                    spread_c(k, d, c).start()

        only(k, finish)

    for o in range(1, peers):
        bias_copy(o).wait()
    total = biases[0]
    for i in range(1, peers):
        total = total + biases[i]
    width = total.shape[1]
    for i in range(8):
        grad_bdec[:, i * width : (i + 1) * width] = total[i : i + 1, :]

    for k in (0, 1):

        @pl.when(receives[k])
        def _():
            for d in range(rows):
                spread_c(k, d, 1 - c).wait_recv()

        @pl.when(forwards[k])
        def _():
            for d in range(rows):
                spread_c(k, d, c).wait_send()

        def drain(k=k):
            for d in range(rows):
                core_copy(k, d).wait_send()
                x_copy(k, d).wait_send()
                spread_x(k, d).wait_send()
                if d:
                    z_copy(k, d).wait_send()
                    spread_z(k, d).wait_send()

        only(k, drain)

    pl.when(bottom)(up.wait_send)
    pl.when(top)(down.wait_send)


def exchange(partial, targets, b_dec, peers):
    depth, tokens, features = partial.shape
    rows = peers // 2
    chunk = tokens // peers
    slots = pltpu.VMEM((2, rows, chunk, features), bf16)
    dma = pltpu.SemaphoreType.DMA((2, rows))
    flat = pltpu.SemaphoreType.DMA((peers,))
    errors, grad_bdec = pl.pallas_call(
        functools.partial(exchange_kernel, rows),
        out_shape=[
            jax.ShapeDtypeStruct((depth, peers, chunk, features), bf16),
            jax.ShapeDtypeStruct((1, features), f32),
        ],
        in_specs=[pl.BlockSpec(memory_space=pltpu.VMEM)] * 3,
        out_specs=[pl.BlockSpec(memory_space=pltpu.VMEM)] * 2,
        scratch_shapes=[
            pltpu.VMEM((2, peers, chunk, features), bf16),
            slots, slots, slots, slots,
            pltpu.VMEM((2, chunk, features), f32),
            pltpu.VMEM((chunk, features), bf16),
            pltpu.VMEM((chunk, features), bf16),
            pltpu.VMEM((peers, 8, features // 8), f32),
        ] + [dma] * 6 + [pltpu.SemaphoreType.DMA((2,))] * 2 + [dma] * 6 + [flat] * 2,
        compiler_params=pltpu.CompilerParams(
            collective_id=1, has_side_effects=True, vmem_limit_bytes=VMEM_LIMIT
        ),
    )(partial.reshape(depth, peers, chunk, features), targets, b_dec)
    return errors.reshape(depth, tokens, features), grad_bdec


def paired(depth, peers, chunk, features):
    layers = lax.axis_size("layer")
    return layers == depth == 4 and peers % 2 == 0 and chunk % 16 == 0 and features % 1024 == 0


def local(inputs, targets, w_enc, b_enc, w_dec, b_dec):
    src = lax.axis_index("layer").astype(jnp.int32)[None]
    peers = lax.axis_size("latent")
    direct = paired(w_dec.shape[1], peers, inputs.shape[1], inputs.shape[2])
    if direct:
        positive, act, partial, whole = joined(inputs[0], w_enc[0], b_enc, w_dec[0], peers)
        errors, grad_bdec = exchange(partial, targets[0], b_dec, peers)
    else:
        whole = lax.all_gather(inputs[0], "latent", axis=0, tiled=True)
        positive, act, partial = forward(src, whole, w_enc[0], b_enc, w_dec[0], f32)
        spread = lax.psum_scatter(partial, "layer", scatter_dimension=0, tiled=True)
        recon = lax.psum_scatter(spread, "latent", scatter_dimension=1, tiled=True)
        error = recon[0] + b_dec[0] - targets[0].astype(f32)
        err_low = error.astype(bf16)[None]
        stacked = lax.all_gather(err_low, "latent", axis=1, tiled=True)
        errors = lax.all_gather(stacked, "layer", axis=0, tiled=True)
        grad_bdec = lax.psum(jnp.sum(error, axis=0), "latent")[None, :]
    grad_enc, grad_benc, grad_dec = backward(src, whole, positive, act, errors, w_dec[0])
    return (grad_enc[None], grad_benc, grad_dec[None], grad_bdec)


def solution(mesh):
    placed = (
        P("layer", "latent", None),
        P("layer", "latent", None),
        P("layer", None, "latent"),
        P("layer", "latent"),
        P("layer", None, "latent", None),
        P("layer", None),
    )
    return jax.shard_map(
        local,
        mesh=mesh,
        in_specs=placed,
        out_specs=(
            P("layer", None, "latent"),
            P("layer", "latent"),
            P("layer", None, "latent", None),
            P("layer", None),
        ),
        check_vma=False,
    )
```
